256 devices in a mesh: tm: 16 (over y_lo, x, core), col: 16 (over z, y_hi).
Axes of the slice: x: 4, y: 4 (y_hi: 2, y_lo: 2; y = y_hi * 2 + y_lo), z: 8, core: 2. Of those that a mesh axis runs over, the one named last changes fastest.
Arguments:
- panel: bfloat16 [1024, 131072], P('col', 'tm'), may hold values from -60 to 60
- response: float32 [131072], replicated, may hold values from 0.25 to 2.5
Outputs:
- normal: float32 [1024, 1024], P('col', 'tm')
The draws below stay inside these ranges and needn't reach their ends.
All inputs are finite; a program needn't handle non-finite values.
Results may differ from the reference program's by a relative error of at most 0.0015.
Values may be sent and summed in bfloat16 or wider, within the bound.
No kernel may reach another device: no remote copies, remote signals or barrier semaphores. Data moves between devices by JAX's collectives and lax.ppermute only.
A program may use at most 64 MiB of HBM per device.

```python
import math
import jax
import jax.numpy as jnp
from jax import lax

COLS = 1024
EPOCHS = 131072


def draw_panel(key, part):
    key_list = jax.random.split(jax.random.fold_in(key, 7001), 6)
    noise_part = jax.random.truncated_normal(key_list[0], -4.0, 4.0, (COLS, EPOCHS), jnp.float32)
    level_log = jax.random.uniform(key_list[1], (COLS, 64), jnp.float32, math.log(0.3), math.log(3.0))
    levels = jnp.repeat(jnp.exp(level_log), EPOCHS // 64, axis=1)
    tone_freq = jax.random.randint(key_list[2], (16, 1), 1, EPOCHS // 2, jnp.int32)
    epoch_index = jnp.arange(EPOCHS, dtype=jnp.int32)[None, :]
    upper_part = tone_freq * (epoch_index // 256) % EPOCHS
    phase_index = (upper_part * 256 + tone_freq * (epoch_index % 256)) % EPOCHS
    tone_angle = phase_index.astype(jnp.float32) * (2.0 * math.pi / EPOCHS)
    envelope_log = jax.random.uniform(key_list[3], (16, 64), jnp.float32, math.log(0.5), math.log(2.0))
    envelope = jnp.repeat(jnp.exp(envelope_log), EPOCHS // 64, axis=1)
    basis_cos = jnp.cos(tone_angle) * envelope
    basis_sin = jnp.sin(tone_angle) * envelope
    amplitude = 0.35 * jax.random.truncated_normal(key_list[4], -4.0, 4.0, (COLS, 16), jnp.float32)
    offset = jax.random.uniform(key_list[5], (COLS, 16), jnp.float32, -math.pi, math.pi)
    tone_part = jnp.dot(amplitude * jnp.cos(offset), basis_cos, precision=lax.Precision.HIGHEST)
    tone_part = tone_part - jnp.dot(amplitude * jnp.sin(offset), basis_sin, precision=lax.Precision.HIGHEST)
    return (noise_part * levels + tone_part).astype(jnp.bfloat16)


def setup_inputs(seed: int = 0) -> dict:
    seeds = jax.random.split(jax.random.key(seed), 3)
    panel = draw_panel(jax.random.fold_in(seeds[2], 71), 0)
    response = jnp.clip(jnp.exp(jax.random.uniform(seeds[1], (EPOCHS,), jnp.float32, math.log(0.25), math.log(2.5))), 0.25, 2.5)
    return {"panel": panel, "response": response}


def whiten_block(panel_block, response):
    spectrum = jnp.fft.fft(panel_block.astype(jnp.float32), axis=1)
    filtered = jnp.fft.ifft(spectrum * response, axis=1)
    return jnp.real(filtered).astype(jnp.bfloat16)


def reference(panel, response):
    panel_blocks = panel.reshape(COLS // 64, 64, EPOCHS)
    whitened = lax.map(lambda block_rows: whiten_block(block_rows, response), panel_blocks)
    whitened = whitened.reshape(COLS, EPOCHS)
    normal = lax.dot_general(whitened, whitened, (((1,), (1,)), ((), ())), preferred_element_type=jnp.float32)
    return normal / EPOCHS
```

```python
import math

import jax
import jax.numpy as jnp
import numpy as np
from jax import lax
from jax.experimental import pallas as pl
from jax.experimental.pallas import tpu as pltpu
from jax.sharding import Mesh
from jax.sharding import PartitionSpec as P

EPOCHS = 131072
SLOW = 512
FAST = 256
HALF = SLOW // 2
KEPT = HALF + 8
COLUMNS = 4
DEVICES = 256

EVERY = ("z", "yh", "yl", "x", "core")
ROWS = ("z", "yh")
TIMES = ("yl", "x", "core")
CHIPS = ("yl", "x")

F32 = jnp.float32
BF16 = jnp.bfloat16


def split_table(table):
    upper = table.astype(np.float32).astype(BF16)
    lower = (table - upper.astype(np.float64)).astype(np.float32).astype(BF16)
    return upper, lower


def phase(rows, cols, length):
    index = np.outer(np.asarray(rows, np.int64), np.asarray(cols, np.int64)) % length
    return index * (2.0 * math.pi / length)


def host_tables():
    slow = np.arange(SLOW)
    cosine = np.cos(phase(np.arange(HALF + 1), slow, SLOW))
    sine = np.sin(phase(np.arange(1, HALF), slow, SLOW))
    real_fold = np.concatenate([cosine[:HALF], cosine[HALF:], -sine], axis=0)
    turn = phase(np.arange(KEPT), np.arange(FAST), EPOCHS)
    inner = phase(np.arange(FAST), np.arange(FAST), FAST)
    complex_inner = np.block(
        [[np.cos(inner), -np.sin(inner)], [np.sin(inner), np.cos(inner)]]
    )
    odd = 2 * np.arange(HALF) + 1
    spread = np.cos(phase(odd, odd, 8 * HALF)) * math.sqrt(2.0 / HALF)
    spread_upper, _ = split_table(spread)
    norm = math.sqrt(float((spread_upper.astype(np.float64)[0] ** 2).sum()))
    return (
        split_table(real_fold),
        (np.cos(turn).astype(np.float32), np.sin(turn).astype(np.float32)),
        split_table(complex_inner),
        spread_upper,
        norm,
    )


def dot(left, right):
    return jnp.dot(left, right, preferred_element_type=F32)


def deal_kernel(panel_ref, out_ref, spread_ref):
    runs = panel_ref.shape[1] // FAST
    stride = COLUMNS * runs
    for column in range(COLUMNS):
        for run in range(runs):
            for half in range(FAST // 128):
                lane = run * FAST + half * 128
                piece = panel_ref[column * 16 : (column + 1) * 16, lane : lane + 128]
                spread_ref[half, pl.ds(column * runs + run, 16, stride=stride), :] = piece.astype(F32)
    for half in range(FAST // 128):
        out_ref[:, half * 128 : (half + 1) * 128] = spread_ref[half].astype(BF16)


def deal(panel):
    rows, epochs = panel.shape
    runs = epochs // FAST
    return pl.pallas_call(
        deal_kernel,
        out_shape=jax.ShapeDtypeStruct((16 * COLUMNS * runs, FAST), BF16),
        scratch_shapes=[pltpu.VMEM((FAST // 128, 16 * COLUMNS * runs, 128), F32)],
        name="deal",
    )(panel)


def filter_kernel(
    series_ref,
    fold_hi,
    fold_lo,
    turn_cos,
    turn_sin,
    inner_hi,
    inner_lo,
    gain_ref,
    spread,
    out_ref,
    lines_ref,
):
    blocks = series_ref.shape[0]
    runs = SLOW // blocks
    first_row = lax.broadcasted_iota(jnp.int32, (HALF, FAST), 0) == 0
    gain = gain_ref[0:HALF, :]
    edge_gain = gain_ref[HALF : HALF + 1, :]
    tiles = 2 * FAST // 128
    for column in range(COLUMNS):
        series = jnp.concatenate(
            [series_ref[j, column * runs : (column + 1) * runs, :] for j in range(blocks)], axis=0
        )
        folded = dot(fold_hi[...], series) + dot(fold_lo[...], series)
        real = folded[0:HALF]
        imag = folded[HALF:SLOW]
        edge = imag[0:1]
        cosine = turn_cos[0:HALF, :]
        sine = turn_sin[0:HALF, :]
        turned_re = real * cosine + imag * sine
        turned_im = jnp.where(first_row, 0.0, imag * cosine - real * sine)
        edge_re = edge * turn_cos[HALF : HALF + 1, :]
        edge_im = -edge * turn_sin[HALF : HALF + 1, :]
        edge_row = jnp.concatenate([edge_re, edge_im], axis=1)
        turned = jnp.concatenate(
            [
                jnp.concatenate([turned_re, turned_im], axis=1),
                jnp.broadcast_to(edge_row, (16, 2 * FAST)),
            ],
            axis=0,
        )
        upper = turned.astype(BF16)
        lower = (turned - upper.astype(F32)).astype(BF16)
        lines = dot(upper, inner_hi[...]) + dot(upper, inner_lo[...]) + dot(lower, inner_hi[...])
        line_re = lines[0:HALF, 0:FAST] * gain
        line_im = lines[0:HALF, FAST:] * gain
        edge_line = (lines[HALF : HALF + 1, 0:FAST] + lines[HALF : HALF + 1, FAST:]) * edge_gain
        first = line_re + line_im
        line_re = jnp.where(first_row, first, line_re)
        line_im = jnp.where(first_row, jnp.broadcast_to(edge_line, (HALF, FAST)), line_im)
        packed = jnp.concatenate([line_re, line_im], axis=1)
        upper = packed.astype(BF16)
        lower = (packed - upper.astype(F32)).astype(BF16)
        mixed = dot(spread[...], upper) + dot(spread[...], lower)
        for tile in range(tiles):
            lines_ref[pl.ds(column * tiles + tile, HALF, stride=COLUMNS * tiles), :] = mixed[
                :, tile * 128 : (tile + 1) * 128
            ]
    out_ref[...] = lines_ref[...].astype(BF16)


def filter_columns(series, tables, gain):
    (fold_hi, fold_lo), (turn_cos, turn_sin), (inner_hi, inner_lo), spread, _ = tables
    rows = DEVICES * COLUMNS * 2 * FAST // 128
    return pl.pallas_call(
        filter_kernel,
        out_shape=jax.ShapeDtypeStruct((rows, 128), BF16),
        scratch_shapes=[pltpu.VMEM((rows, 128), F32)],
        name="filter",
    )(
        series,
        jnp.asarray(fold_hi),
        jnp.asarray(fold_lo),
        jnp.asarray(turn_cos),
        jnp.asarray(turn_sin),
        jnp.asarray(inner_hi),
        jnp.asarray(inner_lo),
        gain,
        jnp.asarray(spread),
    )


def gather_kernel(lines_ref, out_ref, wide_ref):
    tiles = 2 * FAST // 128
    wide_ref[...] = lines_ref[...].astype(F32)
    for column in range(COLUMNS):
        for tile in range(tiles):
            rows = wide_ref[
                pl.ds(column * tiles + tile, DEVICES, stride=COLUMNS * tiles), :
            ].astype(BF16)
            for b in range(16):
                out_ref[
                    b * 64 + column * 16 : b * 64 + column * 16 + 16, tile * 128 : (tile + 1) * 128
                ] = rows[b * 16 : b * 16 + 16, :]


def gather_rows(lines):
    return pl.pallas_call(
        gather_kernel,
        out_shape=jax.ShapeDtypeStruct((DEVICES * COLUMNS, 2 * FAST), BF16),
        scratch_shapes=[pltpu.VMEM(lines.shape, F32)],
        name="gather_rows",
    )(lines)


def gram_kernel(core_ref, mine_ref, other_ref, out_ref):
    core = core_ref[0]
    nt = (((1,), (1,)), ((), ()))
    for block in range(8):
        start = pl.multiple_of(128 * block + 64 * core, 64)
        own = lax.dot_general(
            mine_ref[pl.ds(start, 64), :], mine_ref[...], nt, preferred_element_type=F32
        )
        own += lax.dot_general(
            other_ref[pl.ds(start, 64), :], other_ref[...], nt, preferred_element_type=F32
        )
        out_ref[block * 64 : (block + 1) * 64, :] = own.astype(BF16)


def gram(core, mine, other):
    return pl.pallas_call(
        gram_kernel,
        out_shape=jax.ShapeDtypeStruct((512, mine.shape[0]), BF16),
        in_specs=[
            pl.BlockSpec(memory_space=pltpu.SMEM),
            pl.BlockSpec(memory_space=pltpu.VMEM),
            pl.BlockSpec(memory_space=pltpu.VMEM),
        ],
        name="gram",
    )(core, mine, other)


def fold_kernel(parts_ref, out_ref):
    total = parts_ref[0].astype(F32)
    for chip in range(1, parts_ref.shape[0]):
        total += parts_ref[chip].astype(F32)
    lane = lax.broadcasted_iota(jnp.int32, (32, 128), 1) < 64
    for pair in range(8):
        upper = total[0:32, pair * 128 : (pair + 1) * 128]
        lower = total[32:64, pair * 128 : (pair + 1) * 128]
        out_ref[2 * pair] = jnp.where(lane, upper, pltpu.roll(lower, 64, 1))
        out_ref[2 * pair + 1] = jnp.where(lane, pltpu.roll(upper, 64, 1), lower)


def fold(parts):
    return pl.pallas_call(
        fold_kernel,
        out_shape=jax.ShapeDtypeStruct((16, 32, 128), F32),
        name="fold",
    )(parts)


def finish_kernel(parts_ref, out_ref):
    total = parts_ref[0]
    for part in range(1, parts_ref.shape[0]):
        total += parts_ref[part]
    block = jnp.concatenate([total[:, 0:64], total[:, 64:128]], axis=0)
    out_ref[...] = block.T


def finish(parts):
    return pl.pallas_call(
        finish_kernel,
        out_shape=jax.ShapeDtypeStruct((64, 64), F32),
        name="finish",
    )(parts)


def gain_table(response, norm):
    grid = response.reshape(FAST, SLOW)
    mirror = jnp.concatenate(
        [
            jnp.roll(jnp.flip(grid[:, 0:1], axis=0), 1, axis=0),
            jnp.flip(grid[:, HALF : SLOW], axis=(0, 1)),
        ],
        axis=1,
    )
    even = (grid[:, : HALF + 1] + mirror) * 0.5
    weight = np.full((1, HALF + 1), math.sqrt(2.0))
    weight[0, 0] = weight[0, HALF] = 1.0
    even = even * jnp.asarray((weight / (EPOCHS * norm)).astype(np.float32))
    return jnp.pad(even.T, ((0, KEPT - HALF - 1), (0, 0)))


def exchange(values, axes):
    return lax.all_to_all(values, axes, split_axis=0, concat_axis=0, tiled=True)


def on_device(panel, response):
    tables = host_tables()
    gain = gain_table(response, tables[4])
    dealt = deal(panel).reshape(16, -1, FAST)
    series = exchange(dealt, TIMES)
    lines = filter_columns(series, tables, gain)
    lines = exchange(lines.reshape(DEVICES, -1, 128), EVERY).reshape(lines.shape)
    mine = gather_rows(lines)
    other = lax.ppermute(mine, "core", [(0, 1), (1, 0)])
    core = lax.axis_index("core").astype(jnp.int32).reshape(1)
    part = gram(core, mine, other)
    parts = exchange(part.reshape(8, 64, -1), CHIPS)
    folded = exchange(fold(parts), ROWS)
    return finish(folded)


def solution(mesh):
    fine = Mesh(mesh.devices.reshape(2, 4, 2, 8, 2), ("yl", "x", "core", "z", "yh"))
    return jax.shard_map(
        on_device,
        mesh=fine,
        in_specs=(P(ROWS, TIMES), P()),
        out_specs=P(ROWS, TIMES),
        check_vma=False,
    )
```

```python
import math

import jax
import jax.numpy as jnp
import numpy as np
from jax import lax
from jax.experimental import pallas as pl
from jax.experimental.pallas import tpu as pltpu
from jax.sharding import Mesh
from jax.sharding import PartitionSpec as P

EPOCHS = 131072
SLOW = 512
FAST = 256
HALF = SLOW // 2
KEPT = HALF + 8
CHUNKS = 1
DEVICES = 256
MIB = 1 << 20
FILTER_VMEM = 24 * MIB
GRAM_VMEM = 24 * MIB
FOLD_VMEM = 16 * MIB

EVERY = ("z", "yh", "yl", "x", "core")
ROWS = ("z", "yh")
TIMES = ("yl", "x", "core")
CHIPS = ("yl", "x")

F32 = jnp.float32
BF16 = jnp.bfloat16


def split_table(table):
    upper = table.astype(np.float32).astype(BF16)
    lower = (table - upper.astype(np.float64)).astype(np.float32).astype(BF16)
    return upper, lower


def phase(rows, cols, length):
    index = np.outer(np.asarray(rows, np.int64), np.asarray(cols, np.int64)) % length
    return index * (2.0 * math.pi / length)


def host_tables():
    slow = np.arange(SLOW)
    cosine = np.cos(phase(np.arange(HALF + 1), slow, SLOW))
    sine = np.sin(phase(np.arange(1, HALF), slow, SLOW))
    real_fold = np.concatenate([cosine[:HALF], cosine[HALF:], -sine], axis=0)
    turn = phase(np.arange(KEPT), np.arange(FAST), EPOCHS)
    inner = phase(np.arange(FAST), np.arange(FAST), FAST)
    complex_inner = np.block(
        [[np.cos(inner), -np.sin(inner)], [np.sin(inner), np.cos(inner)]]
    )
    odd = 2 * np.arange(HALF) + 1
    spread = np.cos(phase(odd, odd, 8 * HALF)) * math.sqrt(2.0 / HALF)
    spread_upper, _ = split_table(spread)
    norm = math.sqrt(float((spread_upper.astype(np.float64)[0] ** 2).sum()))
    return (
        split_table(real_fold),
        (np.cos(turn).astype(np.float32), np.sin(turn).astype(np.float32)),
        split_table(complex_inner),
        spread_upper,
        norm,
    )


def dot(left, right):
    return jnp.dot(left, right, preferred_element_type=F32)


def join(parts, axis):
    return jnp.concatenate(parts, axis=axis)


def filter_kernel(
    series_ref,
    fold_hi,
    fold_lo,
    turn_cos,
    turn_sin,
    inner_hi,
    inner_lo,
    gain_ref,
    spread,
    out_ref,
    lines_ref,
):
    blocks, columns, runs, _ = series_ref.shape
    first_row = lax.broadcasted_iota(jnp.int32, (HALF, FAST), 0) == 0
    gain = gain_ref[0:HALF, :]
    edge_gain = gain_ref[HALF : HALF + 1, :]
    tiles = 2 * FAST // 128
    for column in range(columns):
        series = join([series_ref[j, column] for j in range(blocks)], 0)
        folded = dot(join([fold_hi[...], fold_lo[...]], 1), join([series, series], 0))
        real = folded[0:HALF]
        imag = folded[HALF:SLOW]
        edge = imag[0:1]
        cosine = turn_cos[0:HALF, :]
        sine = turn_sin[0:HALF, :]
        turned_re = real * cosine + imag * sine
        turned_im = jnp.where(first_row, 0.0, imag * cosine - real * sine)
        edge_re = edge * turn_cos[HALF : HALF + 1, :]
        edge_im = -edge * turn_sin[HALF : HALF + 1, :]
        edge_row = jnp.broadcast_to(join([edge_re, edge_im], 1), (16, 2 * FAST))
        turned = join([join([turned_re, turned_im], 1), edge_row], 0)
        upper = turned.astype(BF16)
        lower = (turned - upper.astype(F32)).astype(BF16)
        lines = dot(
            join([upper, upper, lower], 1), join([inner_hi[...], inner_lo[...], inner_hi[...]], 0)
        )
        line_re = lines[0:HALF, 0:FAST] * gain
        line_im = lines[0:HALF, FAST:] * gain
        edge_line = (lines[HALF : HALF + 1, 0:FAST] + lines[HALF : HALF + 1, FAST:]) * edge_gain
        first = line_re + line_im
        line_re = jnp.where(first_row, first, line_re)
        line_im = jnp.where(first_row, jnp.broadcast_to(edge_line, (HALF, FAST)), line_im)
        packed = join([line_re, line_im], 1)
        upper = packed.astype(BF16)
        lower = (packed - upper.astype(F32)).astype(BF16)
        mixed = dot(join([spread[...], spread[...]], 1), join([upper, lower], 0))
        for tile in range(tiles):
            lines_ref[pl.ds(tile * columns + column, HALF, stride=columns * tiles), :] = mixed[
                :, tile * 128 : (tile + 1) * 128
            ]
    out_ref[...] = lines_ref[...].astype(BF16)


def filter_columns(series, tables, gain):
    rows = DEVICES * series.shape[1] * 2 * FAST // 128
    return pl.pallas_call(
        filter_kernel,
        out_shape=jax.ShapeDtypeStruct((rows, 128), BF16),
        scratch_shapes=[pltpu.VMEM((rows, 128), F32)],
        compiler_params=pltpu.CompilerParams(vmem_limit_bytes=FILTER_VMEM),
        cost_estimate=pl.CostEstimate(
            flops=2_000_000_000 * series.shape[1], bytes_accessed=4 * MIB, transcendentals=0
        ),
        name="filter",
    )(series, *tables[:6], gain, tables[6])


def gram_rows(core_ref, ref):
    start = 64 * core_ref[0]
    blocks = [ref[pl.ds(pl.multiple_of(128 * b + start, 64), 64), :] for b in range(8)]
    return join(blocks, 0)


def half_gram(core_ref, ref):
    return lax.dot_general(
        gram_rows(core_ref, ref), ref[...], (((1,), (1,)), ((), ())), preferred_element_type=F32
    )


def gram_mine_kernel(core_ref, mine_ref, out_ref):
    out_ref[...] = half_gram(core_ref, mine_ref)


def gram_other_kernel(core_ref, other_ref, begun_ref, out_ref):
    out_ref[...] = (begun_ref[...] + half_gram(core_ref, other_ref)).astype(BF16)


def gram(kernel, dtype, name, core, *arrays):
    return pl.pallas_call(
        kernel,
        out_shape=jax.ShapeDtypeStruct((512, 1024), dtype),
        in_specs=[pl.BlockSpec(memory_space=pltpu.SMEM)]
        + [pl.BlockSpec(memory_space=pltpu.VMEM)] * len(arrays),
        compiler_params=pltpu.CompilerParams(vmem_limit_bytes=GRAM_VMEM),
        cost_estimate=pl.CostEstimate(
            flops=1_000_000_000, bytes_accessed=4 * MIB, transcendentals=0
        ),
        name=name,
    )(core, *arrays)


def fold_kernel(parts_ref, out_ref):
    total = parts_ref[0].astype(F32)
    for chip in range(1, parts_ref.shape[0]):
        total += parts_ref[chip].astype(F32)
    width = 64 // CHUNKS
    group = lax.broadcasted_iota(jnp.int32, (32, 128), 1) // width
    for b in range(16):
        packed = None
        for half in range(2):
            for chunk in range(CHUNKS):
                lane = chunk * (1024 // CHUNKS) + b * width
                tile = lane // 128 * 128
                piece = total[32 * half : 32 * half + 32, tile : tile + 128]
                target = 64 * half + width * chunk
                shift = (target - (lane - tile)) % 128
                piece = pltpu.roll(piece, shift, 1) if shift else piece
                slot = group == target // width
                packed = piece if packed is None else jnp.where(slot, piece, packed)
        out_ref[b] = packed


def fold(parts):
    return pl.pallas_call(
        fold_kernel,
        out_shape=jax.ShapeDtypeStruct((16, 32, 128), F32),
        compiler_params=pltpu.CompilerParams(vmem_limit_bytes=FOLD_VMEM),
        name="fold",
    )(parts)


def finish_kernel(parts_ref, out_ref):
    total = parts_ref[0]
    for part in range(1, parts_ref.shape[0]):
        total += parts_ref[part]
    block = join([total[:, 0:64], total[:, 64:128]], 0)
    out_ref[...] = block.T


def finish(parts):
    return pl.pallas_call(
        finish_kernel,
        out_shape=jax.ShapeDtypeStruct((64, 64), F32),
        compiler_params=pltpu.CompilerParams(vmem_limit_bytes=FOLD_VMEM),
        name="finish",
    )(parts)


def gain_table(response, norm):
    grid = response.reshape(FAST, SLOW)
    mirror = jnp.concatenate(
        [
            jnp.roll(jnp.flip(grid[:, 0:1], axis=0), 1, axis=0),
            jnp.flip(grid[:, HALF : SLOW], axis=(0, 1)),
        ],
        axis=1,
    )
    even = (grid[:, : HALF + 1] + mirror) * 0.5
    weight = np.full((1, HALF + 1), math.sqrt(2.0))
    weight[0, 0] = weight[0, HALF] = 1.0
    even = even * jnp.asarray((weight / (EPOCHS * norm)).astype(np.float32))
    return jnp.pad(even.T, ((0, KEPT - HALF - 1), (0, 0)))


def exchange(values, axes):
    return lax.all_to_all(values, axes, split_axis=0, concat_axis=0, tiled=True)


def on_device(panel, response):
    (fold_hi, fold_lo), (turn_cos, turn_sin), (inner_hi, inner_lo), spread, norm = host_tables()
    tables = [
        jnp.asarray(table)
        for table in (fold_hi, fold_lo, turn_cos, turn_sin, inner_hi, inner_lo, spread)
    ]
    gain = gain_table(response, norm)
    tiles = 2 * FAST // 128
    rows = panel.shape[0] // CHUNKS
    columns = rows // 16
    series = []
    for chunk in range(CHUNKS):
        part = panel[chunk * rows : (chunk + 1) * rows].reshape(16, columns, -1, FAST)
        series.append(exchange(part, TIMES))
    lines = []
    for part in series:
        part = filter_columns(part, tables, gain)
        lines.append(exchange(part.reshape(DEVICES, tiles * columns, 128), EVERY))
    mine = lines[0].reshape(DEVICES, tiles, columns, 128).transpose(0, 2, 1, 3)
    mine = mine.reshape(DEVICES * columns, 2 * FAST)
    other = lax.ppermute(mine, "core", [(0, 1), (1, 0)])
    core = lax.axis_index("core").astype(jnp.int32).reshape(1)
    begun = gram(gram_mine_kernel, F32, "gram_mine", core, mine)
    part = gram(gram_other_kernel, BF16, "gram_other", core, other, begun)
    parts = exchange(part.reshape(8, 64, -1), CHIPS)
    folded = exchange(fold(parts), ROWS)
    return finish(folded)


def solution(mesh):
    fine = Mesh(mesh.devices.reshape(2, 4, 2, 8, 2), ("yl", "x", "core", "z", "yh"))
    return jax.shard_map(
        on_device,
        mesh=fine,
        in_specs=(P(ROWS, TIMES), P()),
        out_specs=P(ROWS, TIMES),
        check_vma=False,
    )
```

```python
import math

import jax
import jax.numpy as jnp
import numpy as np
from jax import lax
from jax.experimental import pallas as pl
from jax.experimental.pallas import tpu as pltpu
from jax.sharding import Mesh
from jax.sharding import PartitionSpec as P

EPOCHS = 131072
SLOW = 512
FAST = 256
HALF = SLOW // 2
KEPT = HALF + 8
DEVICES = 256
MIB = 1 << 20
FILTER_VMEM = 16 * MIB
GRAM_VMEM = 24 * MIB
FOLD_VMEM = 16 * MIB

EVERY = ("z", "yh", "yl", "x", "core")
ROWS = ("z", "yh")
TIMES = ("yl", "x", "core")
PLANE = ("yl", "x", "yh")

F32 = jnp.float32
BF16 = jnp.bfloat16


def split_table(table):
    upper = table.astype(np.float32).astype(BF16)
    lower = (table - upper.astype(np.float64)).astype(np.float32).astype(BF16)
    return upper, lower


def phase(rows, cols, length):
    index = np.outer(np.asarray(rows, np.int64), np.asarray(cols, np.int64)) % length
    return index * (2.0 * math.pi / length)


def host_tables():
    slow = np.arange(SLOW)
    cosine = np.cos(phase(np.arange(HALF + 1), slow, SLOW))
    sine = np.sin(phase(np.arange(1, HALF), slow, SLOW))
    real_fold = np.concatenate([cosine[:HALF], cosine[HALF:], -sine], axis=0)
    turn = phase(np.arange(KEPT), np.arange(FAST), EPOCHS)
    inner = phase(np.arange(FAST), np.arange(FAST), FAST)
    cosine, sine = np.cos(inner), np.sin(inner)
    inner = np.concatenate([cosine, sine - cosine, cosine + sine], axis=1)
    odd = 2 * np.arange(HALF) + 1
    spread = np.cos(phase(odd, odd, 8 * HALF)) * math.sqrt(2.0 / HALF)
    spread_upper, _ = split_table(spread)
    norm = math.sqrt(float((spread_upper.astype(np.float64)[0] ** 2).sum()))
    return (
        split_table(real_fold),
        (np.cos(turn).astype(np.float32), np.sin(turn).astype(np.float32)),
        split_table(inner),
        spread_upper,
        norm,
    )


def dot(left, right):
    return jnp.dot(left, right, preferred_element_type=F32)


def join(parts, axis):
    return jnp.concatenate(parts, axis=axis)


def settle_kernel(table_ref, after_ref, out_ref):
    del table_ref, after_ref, out_ref


def settle(table, after):
    return pl.pallas_call(
        settle_kernel,
        out_shape=jax.ShapeDtypeStruct(table.shape, table.dtype),
        in_specs=[pl.BlockSpec(memory_space=pl.ANY)] * 2,
        out_specs=pl.BlockSpec(memory_space=pl.ANY),
        input_output_aliases={0: 0},
        compiler_params=pltpu.CompilerParams(vmem_limit_bytes=FOLD_VMEM),
        name="settle",
    )(table, after)


def filter_kernel(
    series_ref,
    fold_ref,
    inner_ref,
    turn_ref,
    gain_ref,
    out_ref,
    lines_ref,
):
    fold_hi, fold_lo = fold_ref.at[0:SLOW], fold_ref.at[SLOW : 2 * SLOW]
    spread = fold_ref.at[2 * SLOW : 2 * SLOW + HALF]
    inner_hi, inner_lo = inner_ref.at[0:FAST], inner_ref.at[FAST : 2 * FAST]
    turn_cos, turn_sin = turn_ref.at[0:KEPT], turn_ref.at[KEPT : 2 * KEPT]
    blocks, columns, runs, _ = series_ref.shape
    first_row = lax.broadcasted_iota(jnp.int32, (HALF, FAST), 0) == 0
    gain = gain_ref[0:HALF, :]
    edge_gain = gain_ref[HALF : HALF + 1, :]
    tiles = 2 * FAST // 128
    for column in range(columns):
        series = join([series_ref[j, column] for j in range(blocks)], 0)
        folded = dot(join([fold_hi[...], fold_lo[...]], 1), join([series, series], 0))
        real = folded[0:HALF]
        imag = folded[HALF:SLOW]
        edge = imag[0:1]
        cosine = turn_cos[0:HALF, :]
        sine = turn_sin[0:HALF, :]
        turned_re = real * cosine + imag * sine
        turned_im = jnp.where(first_row, 0.0, imag * cosine - real * sine)
        edge_re = edge * turn_cos[HALF : HALF + 1, :]
        edge_im = -edge * turn_sin[HALF : HALF + 1, :]
        edge_re, edge_im = (jnp.broadcast_to(row, (16, FAST)) for row in (edge_re, edge_im))
        turned_re = join([turned_re, edge_re], 0)
        turned_im = join([turned_im, edge_im], 0)
        products = []
        for index, values in enumerate((turned_re + turned_im, turned_im, turned_re)):
            upper = values.astype(BF16)
            lower = (values - upper.astype(F32)).astype(BF16)
            lanes = slice(index * FAST, (index + 1) * FAST)
            table = join([inner_hi[:, lanes], inner_lo[:, lanes], inner_hi[:, lanes]], 0)
            products.append(dot(join([upper, upper, lower], 1), table))
        line_re = products[0] + products[1]
        line_im = products[0] - products[2]
        edge_line = (line_re[HALF : HALF + 1] + line_im[HALF : HALF + 1]) * edge_gain
        line_re = line_re[0:HALF] * gain
        line_im = line_im[0:HALF] * gain
        first = line_re + line_im
        line_re = jnp.where(first_row, first, line_re)
        line_im = jnp.where(first_row, jnp.broadcast_to(edge_line, (HALF, FAST)), line_im)
        packed = join([line_re, line_im], 1)
        upper = packed.astype(BF16)
        lower = (packed - upper.astype(F32)).astype(BF16)
        mixed = dot(spread[...], join([upper, lower], 0))
        for tile in range(tiles):
            lines_ref[pl.ds(column * tiles + tile, HALF, stride=columns * tiles), :] = mixed[
                :, tile * 128 : (tile + 1) * 128
            ]
    out_ref[...] = lines_ref[...].astype(BF16)


def filter_columns(series, tables, gain):
    rows = DEVICES * series.shape[1] * 2 * FAST // 128
    return pl.pallas_call(
        filter_kernel,
        out_shape=jax.ShapeDtypeStruct((rows, 128), BF16),
        scratch_shapes=[pltpu.VMEM((rows, 128), F32)],
        compiler_params=pltpu.CompilerParams(vmem_limit_bytes=FILTER_VMEM),
        cost_estimate=pl.CostEstimate(
            flops=2_000_000_000 * series.shape[1], bytes_accessed=4 * MIB, transcendentals=0
        ),
        name="filter",
    )(series, *tables, gain)


def half_gram(core_ref, ref):
    start = 64 * core_ref[0]
    left = [ref[pl.ds(pl.multiple_of(128 * b + start, 64), 64), :] for b in range(8)]
    right = [ref[64 * b : 64 * b + 64, :] for b in (*range(0, 16, 2), *range(1, 16, 2))]
    return lax.dot_general(
        join(left, 0), join(right, 0), (((1,), (1,)), ((), ())), preferred_element_type=F32
    )


def gram_mine_kernel(core_ref, mine_ref, out_ref):
    out_ref[...] = half_gram(core_ref, mine_ref)


def gram_other_kernel(core_ref, other_ref, begun_ref, out_ref):
    total = (begun_ref[...] + half_gram(core_ref, other_ref)).astype(BF16)
    for block in range(8):
        for parity in range(2):
            out_ref[2 * block + parity] = total[
                64 * block : 64 * block + 64, 512 * parity : 512 * parity + 512
            ]


def gram(kernel, shape, dtype, name, core, *arrays):
    return pl.pallas_call(
        kernel,
        out_shape=jax.ShapeDtypeStruct(shape, dtype),
        in_specs=[pl.BlockSpec(memory_space=pltpu.SMEM)]
        + [pl.BlockSpec(memory_space=pltpu.VMEM)] * len(arrays),
        compiler_params=pltpu.CompilerParams(vmem_limit_bytes=GRAM_VMEM),
        cost_estimate=pl.CostEstimate(
            flops=1_000_000_000, bytes_accessed=4 * MIB, transcendentals=0
        ),
        name=name,
    )(core, *arrays)


def fold_kernel(parts_ref, out_ref):
    total = parts_ref[0].astype(F32)
    for chip in range(1, parts_ref.shape[0]):
        total += parts_ref[chip].astype(F32)
    lane = lax.broadcasted_iota(jnp.int32, (32, 128), 1) < 64
    for pair in range(4):
        upper = total[0:32, pair * 128 : (pair + 1) * 128]
        lower = total[32:64, pair * 128 : (pair + 1) * 128]
        out_ref[2 * pair] = jnp.where(lane, upper, pltpu.roll(lower, 64, 1))
        out_ref[2 * pair + 1] = jnp.where(lane, pltpu.roll(upper, 64, 1), lower)


def fold(parts):
    return pl.pallas_call(
        fold_kernel,
        out_shape=jax.ShapeDtypeStruct((8, 32, 128), F32),
        compiler_params=pltpu.CompilerParams(vmem_limit_bytes=FOLD_VMEM),
        name="fold",
    )(parts)


def finish_kernel(parts_ref, out_ref):
    total = parts_ref[0]
    for part in range(1, parts_ref.shape[0]):
        total += parts_ref[part]
    block = join([total[:, 0:64], total[:, 64:128]], 0)
    out_ref[...] = block.T


def finish(parts):
    return pl.pallas_call(
        finish_kernel,
        out_shape=jax.ShapeDtypeStruct((64, 64), F32),
        compiler_params=pltpu.CompilerParams(vmem_limit_bytes=FOLD_VMEM),
        name="finish",
    )(parts)


def gain_table(response, norm):
    grid = response.reshape(FAST, SLOW)
    mirror = jnp.concatenate(
        [
            jnp.roll(jnp.flip(grid[:, 0:1], axis=0), 1, axis=0),
            jnp.flip(grid[:, HALF : SLOW], axis=(0, 1)),
        ],
        axis=1,
    )
    even = (grid[:, : HALF + 1] + mirror) * 0.5
    weight = np.full((1, HALF + 1), math.sqrt(2.0))
    weight[0, 0] = weight[0, HALF] = 1.0
    even = even * jnp.asarray((weight / (EPOCHS * norm)).astype(np.float32))
    return jnp.pad(even.T, ((0, KEPT - HALF - 1), (0, 0)))


def exchange(values, axes):
    return lax.all_to_all(values, axes, split_axis=0, concat_axis=0, tiled=True)


def on_device(panel, response):
    fold_tables, turn_tables, inner_tables, spread, norm = host_tables()
    tables = (
        [*fold_tables, np.concatenate([spread, spread], axis=1)],
        inner_tables,
        turn_tables,
    )
    tables = [jnp.asarray(np.concatenate(table)) for table in tables]
    gain = gain_table(response, norm)
    tables = tuple(settle(table, gain) for table in tables)
    tiles = 2 * FAST // 128
    columns = panel.shape[0] // 16
    series = exchange(panel.reshape(16, columns, -1, FAST), TIMES)
    lines = filter_columns(series, tables, gain)
    lines = exchange(lines.reshape(DEVICES, tiles * columns, 128), EVERY)
    mine = lines.reshape(DEVICES * columns, 2 * FAST)
    other = lax.ppermute(mine, "core", [(0, 1), (1, 0)])
    core = lax.axis_index("core").astype(jnp.int32).reshape(1)
    begun = gram(gram_mine_kernel, (512, 1024), F32, "gram_mine", core, mine)
    part = gram(gram_other_kernel, (16, 64, 512), BF16, "gram_other", core, other, begun)
    folded = exchange(fold(exchange(part, PLANE)), ("z",))
    return finish(folded)


def solution(mesh):
    fine = Mesh(mesh.devices.reshape(2, 4, 2, 8, 2), ("yl", "x", "core", "z", "yh"))
    return jax.shard_map(
        on_device,
        mesh=fine,
        in_specs=(P(ROWS, TIMES), P()),
        out_specs=P(ROWS, TIMES),
        check_vma=False,
    )
```

```python
import math

import jax
import jax.numpy as jnp
import numpy as np
from jax import lax
from jax.experimental import pallas as pl
from jax.experimental.pallas import tpu as pltpu
from jax.sharding import Mesh
from jax.sharding import PartitionSpec as P

EPOCHS = 131072
SLOW = 512
FAST = 256
HALF = SLOW // 2
KEPT = HALF + 8
DEVICES = 256
MIB = 1 << 20
FILTER_VMEM = 10 * MIB
GRAM_VMEM = 24 * MIB
FOLD_VMEM = 16 * MIB

EVERY = ("z", "yh", "yl", "x", "core")
ROWS = ("z", "yh")
TIMES = ("yl", "x", "core")
PLANE = ("yh", "yl", "x")

F32 = jnp.float32
BF16 = jnp.bfloat16
F8 = jnp.float8_e5m2
SHIFT = 256.0


def split_table(table):
    upper = table.astype(np.float32).astype(BF16)
    lower = (table - upper.astype(np.float64)).astype(np.float32).astype(BF16)
    return upper, lower


def coarse(table):
    return np.asarray(table, np.float32).astype(F8)


def phase(rows, cols, length):
    index = np.outer(np.asarray(rows, np.int64), np.asarray(cols, np.int64)) % length
    return index * (2.0 * math.pi / length)


def host_tables():
    slow = np.arange(SLOW)
    cosine = np.cos(phase(np.arange(HALF + 1), slow, SLOW))
    sine = np.sin(phase(np.arange(1, HALF), slow, SLOW))
    real_fold = np.concatenate([cosine[:HALF], cosine[HALF:], -sine], axis=0)
    turn = phase(np.arange(KEPT), np.arange(FAST), EPOCHS)
    inner = phase(np.arange(FAST), np.arange(FAST), FAST)
    cosine, sine = np.cos(inner), np.sin(inner)
    inner = np.concatenate([cosine, sine - cosine, cosine + sine], axis=1)
    odd = 2 * np.arange(HALF) + 1
    spread = np.cos(phase(odd, odd, 8 * HALF)) * math.sqrt(2.0 / HALF)
    spread_upper, _ = split_table(spread)
    norm = math.sqrt(float((spread_upper.astype(np.float64)[0] ** 2).sum()))
    return (
        split_table(real_fold),
        (np.cos(turn).astype(np.float32), np.sin(turn).astype(np.float32)),
        split_table(inner),
        spread_upper,
        norm,
    )


def dot(left, right):
    return jnp.dot(left, right, preferred_element_type=F32)


def join(parts, axis):
    return jnp.concatenate(parts, axis=axis)


def settle_kernel(table_ref, after_ref, out_ref):
    del table_ref, after_ref, out_ref


def settle(table, after):
    return pl.pallas_call(
        settle_kernel,
        out_shape=jax.ShapeDtypeStruct(table.shape, table.dtype),
        in_specs=[pl.BlockSpec(memory_space=pl.ANY)] * 2,
        out_specs=pl.BlockSpec(memory_space=pl.ANY),
        input_output_aliases={0: 0},
        compiler_params=pltpu.CompilerParams(vmem_limit_bytes=MIB),
        name="settle",
    )(table, after)


def filter_kernel(
    series_ref,
    fold_ref,
    inner_ref,
    coarse_ref,
    rest_ref,
    turn_ref,
    gain_ref,
    out_ref,
    lines_ref,
):
    fold_hi, fold_lo = fold_ref, coarse_ref.at[0:SLOW]
    spread, spread_lo = inner_ref.at[:, 0:FAST], coarse_ref.at[SLOW : SLOW + HALF, 0:FAST]
    inner_hi = inner_ref.at[:, FAST : 4 * FAST]
    inner_lo = rest_ref
    turn_cos, turn_sin = turn_ref.at[0:KEPT], turn_ref.at[KEPT : 2 * KEPT]
    blocks, columns, runs, _ = series_ref.shape
    first_row = lax.broadcasted_iota(jnp.int32, (HALF, FAST), 0) == 0
    gain = gain_ref[0:HALF, :]
    edge_gain = gain_ref[HALF : HALF + 1, :]
    tiles = 2 * FAST // 128
    for column in range(columns):
        series = join([series_ref[j, column] for j in range(blocks)], 0)
        folded = dot(fold_hi[...], series)
        folded += dot(fold_lo[...], series.astype(F32).astype(F8)) * (1 / SHIFT)
        real = folded[0:HALF]
        imag = folded[HALF:SLOW]
        edge = imag[0:1]
        cosine = turn_cos[0:HALF, :]
        sine = turn_sin[0:HALF, :]
        turned_re = real * cosine + imag * sine
        turned_im = jnp.where(first_row, 0.0, imag * cosine - real * sine)
        edge_re = edge * turn_cos[HALF : HALF + 1, :]
        edge_im = -edge * turn_sin[HALF : HALF + 1, :]
        edge_re, edge_im = (jnp.broadcast_to(row, (16, FAST)) for row in (edge_re, edge_im))
        turned_re = join([turned_re, edge_re], 0)
        turned_im = join([turned_im, edge_im], 0)
        products = []
        for index, values in enumerate((turned_re + turned_im, turned_im, turned_re)):
            upper = values.astype(BF16)
            lower = ((values - upper.astype(F32)) * SHIFT).astype(F8)
            lanes = slice(index * FAST, (index + 1) * FAST)
            product = dot(upper, inner_hi[:, lanes])
            coarse_values = join([upper.astype(F32).astype(F8), lower], 1)
            products.append(product + dot(coarse_values, inner_lo[:, lanes]) * (1 / SHIFT))
        line_re = products[0] + products[1]
        line_im = products[0] - products[2]
        edge_line = (line_re[HALF : HALF + 1] + line_im[HALF : HALF + 1]) * edge_gain
        line_re = line_re[0:HALF] * gain
        line_im = line_im[0:HALF] * gain
        first = line_re + line_im
        line_re = jnp.where(first_row, first, line_re)
        line_im = jnp.where(first_row, jnp.broadcast_to(edge_line, (HALF, FAST)), line_im)
        packed = join([line_re, line_im], 1)
        upper = packed.astype(BF16)
        lower = ((packed - upper.astype(F32)) * SHIFT).astype(F8)
        mixed = dot(spread[...], upper) + dot(spread_lo[...], lower) * (1 / SHIFT)
        for tile in range(tiles):
            lines_ref[pl.ds(column * tiles + tile, HALF, stride=columns * tiles), :] = mixed[
                :, tile * 128 : (tile + 1) * 128
            ]
    out_ref[...] = lines_ref[...].astype(BF16)


def filter_columns(series, tables, gain):
    rows = DEVICES * series.shape[1] * 2 * FAST // 128
    return pl.pallas_call(
        filter_kernel,
        out_shape=jax.ShapeDtypeStruct((rows, 128), BF16),
        scratch_shapes=[pltpu.VMEM((rows, 128), F32)],
        compiler_params=pltpu.CompilerParams(vmem_limit_bytes=FILTER_VMEM),
        cost_estimate=pl.CostEstimate(
            flops=2_000_000_000 * series.shape[1], bytes_accessed=4 * MIB, transcendentals=0
        ),
        name="filter",
    )(series, *tables, gain)


def half_gram(core_ref, ref):
    start = 64 * core_ref[0]
    left = [ref[pl.ds(pl.multiple_of(128 * b + start, 64), 64), :] for b in range(8)]
    right = [ref[64 * b : 64 * b + 64, :] for b in (*range(0, 16, 2), *range(1, 16, 2))]
    return lax.dot_general(
        join(left, 0), join(right, 0), (((1,), (1,)), ((), ())), preferred_element_type=F32
    )


def gram_mine_kernel(core_ref, mine_ref, out_ref):
    out_ref[...] = half_gram(core_ref, mine_ref)


def gram_other_kernel(core_ref, other_ref, begun_ref, out_ref):
    total = (begun_ref[...] + half_gram(core_ref, other_ref)).astype(BF16)
    for block in range(8):
        for parity in range(2):
            out_ref[8 * parity + block] = total[
                64 * block : 64 * block + 64, 512 * parity : 512 * parity + 512
            ]


def gram(kernel, shape, dtype, name, core, *arrays):
    return pl.pallas_call(
        kernel,
        out_shape=jax.ShapeDtypeStruct(shape, dtype),
        in_specs=[pl.BlockSpec(memory_space=pltpu.SMEM)]
        + [pl.BlockSpec(memory_space=pltpu.VMEM)] * len(arrays),
        compiler_params=pltpu.CompilerParams(vmem_limit_bytes=GRAM_VMEM),
        cost_estimate=pl.CostEstimate(
            flops=1_000_000_000, bytes_accessed=4 * MIB, transcendentals=0
        ),
        name=name,
    )(core, *arrays)


def fold_kernel(parts_ref, out_ref):
    total = parts_ref[0].astype(F32)
    for chip in range(1, parts_ref.shape[0]):
        total += parts_ref[chip].astype(F32)
    lane = lax.broadcasted_iota(jnp.int32, (32, 128), 1) < 64
    for pair in range(4):
        upper = total[0:32, pair * 128 : (pair + 1) * 128]
        lower = total[32:64, pair * 128 : (pair + 1) * 128]
        out_ref[2 * pair] = jnp.where(lane, upper, pltpu.roll(lower, 64, 1))
        out_ref[2 * pair + 1] = jnp.where(lane, pltpu.roll(upper, 64, 1), lower)


def fold(parts):
    return pl.pallas_call(
        fold_kernel,
        out_shape=jax.ShapeDtypeStruct((8, 32, 128), F32),
        compiler_params=pltpu.CompilerParams(vmem_limit_bytes=FOLD_VMEM),
        name="fold",
    )(parts)


def finish_kernel(parts_ref, out_ref):
    total = parts_ref[0]
    for part in range(1, parts_ref.shape[0]):
        total += parts_ref[part]
    block = join([total[:, 0:64], total[:, 64:128]], 0)
    out_ref[...] = block.T


def finish(parts):
    return pl.pallas_call(
        finish_kernel,
        out_shape=jax.ShapeDtypeStruct((64, 64), F32),
        compiler_params=pltpu.CompilerParams(vmem_limit_bytes=FOLD_VMEM),
        name="finish",
    )(parts)


def gain_table(response, norm):
    grid = response.reshape(FAST, SLOW)
    mirror = jnp.concatenate(
        [
            jnp.roll(jnp.flip(grid[:, 0:1], axis=0), 1, axis=0),
            jnp.flip(grid[:, HALF : SLOW], axis=(0, 1)),
        ],
        axis=1,
    )
    even = (grid[:, : HALF + 1] + mirror) * 0.5
    weight = np.full((1, HALF + 1), math.sqrt(2.0))
    weight[0, 0] = weight[0, HALF] = 1.0
    even = even * jnp.asarray((weight / (EPOCHS * norm)).astype(np.float32))
    return jnp.pad(even.T, ((0, KEPT - HALF - 1), (0, 0)))


def exchange(values, axes):
    return lax.all_to_all(values, axes, split_axis=0, concat_axis=0, tiled=True)


def on_device(panel, response):
    fold_tables, turn_tables, inner_tables, spread, norm = host_tables()
    (fold_hi, fold_lo), (inner_hi, inner_lo) = fold_tables, inner_tables
    tables = (
        fold_hi,
        np.concatenate([spread, inner_hi], axis=1),
        np.concatenate([coarse(np.asarray(fold_lo, np.float32) * SHIFT), np.tile(coarse(spread), (1, 2))]),
        np.concatenate([coarse(np.asarray(inner_lo, np.float32) * SHIFT), coarse(inner_hi)]),
        np.concatenate(turn_tables),
    )
    tables = [jnp.asarray(table) for table in tables]
    gain = gain_table(response, norm)
    tables = tuple(settle(table, gain) for table in tables)
    tiles = 2 * FAST // 128
    columns = panel.shape[0] // 16
    series = exchange(panel.reshape(16, columns, -1, FAST), TIMES)
    lines = filter_columns(series, tables, gain)
    lines = exchange(lines.reshape(DEVICES, tiles * columns, 128), EVERY)
    mine = lines.reshape(DEVICES * columns, 2 * FAST)
    other = lax.ppermute(mine, "core", [(0, 1), (1, 0)])
    core = lax.axis_index("core").astype(jnp.int32).reshape(1)
    begun = gram(gram_mine_kernel, (512, 1024), F32, "gram_mine", core, mine)
    part = gram(gram_other_kernel, (16, 64, 512), BF16, "gram_other", core, other, begun)
    folded = exchange(fold(exchange(part, PLANE)), ("z",))
    return finish(folded)


def solution(mesh):
    fine = Mesh(mesh.devices.reshape(2, 4, 2, 8, 2), ("yl", "x", "core", "z", "yh"))
    return jax.shard_map(
        on_device,
        mesh=fine,
        in_specs=(P(ROWS, TIMES), P()),
        out_specs=P(ROWS, TIMES),
        check_vma=False,
    )
```

```python
import math

import jax
import jax.numpy as jnp
import numpy as np
from jax import lax
from jax.experimental import pallas as pl
from jax.experimental.pallas import tpu as pltpu
from jax.sharding import Mesh
from jax.sharding import PartitionSpec as P

EPOCHS = 131072
SLOW = 512
FAST = 256
HALF = SLOW // 2
KEPT = HALF + 8
DEVICES = 256
MIB = 1 << 20
FILTER_VMEM = 10 * MIB
GRAM_VMEM = 24 * MIB
FOLD_VMEM = 16 * MIB

EVERY = ("z", "yh", "yl", "x", "core")
ROWS = ("z", "yh")
TIMES = ("yl", "x", "core")
PLANE = ("yh", "x", "yl")

F32 = jnp.float32
BF16 = jnp.bfloat16
F8 = jnp.float8_e5m2
SHIFT = 256.0


def split_table(table):
    upper = table.astype(np.float32).astype(BF16)
    lower = (table - upper.astype(np.float64)).astype(np.float32).astype(BF16)
    return upper, lower


def coarse(table):
    return np.asarray(table, np.float32).astype(F8)


def phase(rows, cols, length):
    index = np.outer(np.asarray(rows, np.int64), np.asarray(cols, np.int64)) % length
    return index * (2.0 * math.pi / length)


def host_tables():
    slow = np.arange(SLOW)
    cosine = np.cos(phase(np.arange(HALF + 1), slow, SLOW))
    sine = np.sin(phase(np.arange(1, HALF), slow, SLOW))
    real_fold = np.concatenate([cosine[:HALF], cosine[HALF:], -sine], axis=0)
    turn = phase(np.arange(KEPT), np.arange(FAST), EPOCHS)
    inner = phase(np.arange(FAST), np.arange(FAST), FAST)
    cosine, sine = np.cos(inner), np.sin(inner)
    inner = np.concatenate([cosine, sine - cosine, cosine + sine], axis=1)
    odd = 2 * np.arange(HALF) + 1
    spread = np.cos(phase(odd, odd, 8 * HALF)) * math.sqrt(2.0 / HALF)
    spread_upper, _ = split_table(spread)
    norm = math.sqrt(float((spread_upper.astype(np.float64)[0] ** 2).sum()))
    return (
        split_table(real_fold),
        (np.cos(turn).astype(np.float32), np.sin(turn).astype(np.float32)),
        split_table(inner),
        spread_upper,
        norm,
    )


def dot(left, right):
    return jnp.dot(left, right, preferred_element_type=F32)


def join(parts, axis):
    return jnp.concatenate(parts, axis=axis)


def settle_kernel(table_ref, after_ref, out_ref):
    del table_ref, after_ref, out_ref


def settle(table, after):
    return pl.pallas_call(
        settle_kernel,
        out_shape=jax.ShapeDtypeStruct(table.shape, table.dtype),
        in_specs=[pl.BlockSpec(memory_space=pl.ANY)] * 2,
        out_specs=pl.BlockSpec(memory_space=pl.ANY),
        input_output_aliases={0: 0},
        compiler_params=pltpu.CompilerParams(vmem_limit_bytes=MIB),
        name="settle",
    )(table, after)


def filter_kernel(
    series_ref,
    fold_ref,
    inner_ref,
    coarse_ref,
    rest_ref,
    turn_ref,
    gain_ref,
    out_ref,
):
    fold_hi, fold_lo = fold_ref, coarse_ref.at[0:SLOW]
    spread, spread_lo = inner_ref.at[:, 0:FAST], coarse_ref.at[SLOW : SLOW + HALF, 0:FAST]
    inner_hi = inner_ref.at[:, FAST : 4 * FAST]
    inner_lo = rest_ref
    turn_cos, turn_sin = turn_ref.at[0:KEPT], turn_ref.at[KEPT : 2 * KEPT]
    blocks, columns, runs, _ = series_ref.shape
    first_row = lax.broadcasted_iota(jnp.int32, (HALF, FAST), 0) == 0
    gain = gain_ref[0:HALF, :]
    edge_gain = gain_ref[HALF : HALF + 1, :]
    for column in range(columns):
        series = join([series_ref[j, column] for j in range(blocks)], 0)
        folded = dot(fold_hi[...], series)
        folded += dot(fold_lo[...], series.astype(F8)) * (1 / SHIFT)
        real = folded[0:HALF]
        imag = folded[HALF:SLOW]
        edge = imag[0:1]
        cosine = turn_cos[0:HALF, :]
        sine = turn_sin[0:HALF, :]
        turned_re = real * cosine + imag * sine
        turned_im = jnp.where(first_row, 0.0, imag * cosine - real * sine)
        edge_re = edge * turn_cos[HALF : HALF + 1, :]
        edge_im = -edge * turn_sin[HALF : HALF + 1, :]
        edge_re, edge_im = (jnp.broadcast_to(row, (16, FAST)) for row in (edge_re, edge_im))
        turned_re = join([turned_re, edge_re], 0)
        turned_im = join([turned_im, edge_im], 0)
        products = []
        for index, values in enumerate((turned_re + turned_im, turned_im, turned_re)):
            upper = values.astype(BF16)
            lower = ((values - upper.astype(F32)) * SHIFT).astype(F8)
            lanes = slice(index * FAST, (index + 1) * FAST)
            product = dot(upper, inner_hi[:, lanes])
            coarse_values = join([values.astype(F8), lower], 1)
            products.append(product + dot(coarse_values, inner_lo[:, lanes]) * (1 / SHIFT))
        line_re = products[0] + products[1]
        line_im = products[0] - products[2]
        edge_line = (line_re[HALF : HALF + 1] + line_im[HALF : HALF + 1]) * edge_gain
        line_re = line_re[0:HALF] * gain
        line_im = line_im[0:HALF] * gain
        first = line_re + line_im
        line_re = jnp.where(first_row, first, line_re)
        line_im = jnp.where(first_row, jnp.broadcast_to(edge_line, (HALF, FAST)), line_im)
        packed = join([line_re, line_im], 1)
        upper = packed.astype(BF16)
        lower = ((packed - upper.astype(F32)) * SHIFT).astype(F8)
        mixed = dot(spread[...], upper) + dot(spread_lo[...], lower) * (1 / SHIFT)
        out_ref[:, 2 * FAST * column : 2 * FAST * (column + 1)] = mixed.astype(BF16)


def filter_columns(series, tables, gain):
    return pl.pallas_call(
        filter_kernel,
        out_shape=jax.ShapeDtypeStruct((DEVICES, series.shape[1] * 2 * FAST), BF16),
        in_specs=[pl.BlockSpec(memory_space=pltpu.VMEM)] * (len(tables) + 2),
        out_specs=pl.BlockSpec(memory_space=pltpu.VMEM),
        compiler_params=pltpu.CompilerParams(vmem_limit_bytes=FILTER_VMEM),
        cost_estimate=pl.CostEstimate(
            flops=2_000_000_000 * series.shape[1], bytes_accessed=4 * MIB, transcendentals=0
        ),
        name="filter",
    )(series, *tables, gain)


def half_gram(core_ref, ref):
    start = 64 * core_ref[0]
    left = [ref[pl.ds(pl.multiple_of(128 * b + start, 64), 64), :] for b in range(8)]
    right = [ref[64 * b : 64 * b + 64, :] for b in (*range(0, 16, 2), *range(1, 16, 2))]
    return lax.dot_general(
        join(left, 0), join(right, 0), (((1,), (1,)), ((), ())), preferred_element_type=F32
    )


def gram_mine_kernel(core_ref, mine_ref, out_ref):
    out_ref[...] = half_gram(core_ref, mine_ref)


def gram_other_kernel(core_ref, other_ref, begun_ref, out_ref):
    total = (begun_ref[...] + half_gram(core_ref, other_ref)).astype(BF16)
    for block in range(8):
        for parity in range(2):
            out_ref[8 * parity + 2 * (block % 4) + block // 4] = total[
                64 * block : 64 * block + 64, 512 * parity : 512 * parity + 512
            ]


def gram(kernel, shape, dtype, name, core, *arrays):
    return pl.pallas_call(
        kernel,
        out_shape=jax.ShapeDtypeStruct(shape, dtype),
        in_specs=[pl.BlockSpec(memory_space=pltpu.SMEM)]
        + [pl.BlockSpec(memory_space=pltpu.VMEM)] * len(arrays),
        out_specs=pl.BlockSpec(memory_space=pltpu.VMEM),
        compiler_params=pltpu.CompilerParams(vmem_limit_bytes=GRAM_VMEM),
        cost_estimate=pl.CostEstimate(
            flops=1_000_000_000, bytes_accessed=4 * MIB, transcendentals=0
        ),
        name=name,
    )(core, *arrays)


def fold_kernel(parts_ref, out_ref):
    total = parts_ref[0].astype(F32)
    for chip in range(1, parts_ref.shape[0]):
        total += parts_ref[chip].astype(F32)
    lane = lax.broadcasted_iota(jnp.int32, (32, 128), 1) < 64
    for pair in range(4):
        upper = total[0:32, pair * 128 : (pair + 1) * 128]
        lower = total[32:64, pair * 128 : (pair + 1) * 128]
        out_ref[2 * pair] = jnp.where(lane, upper, pltpu.roll(lower, 64, 1))
        out_ref[2 * pair + 1] = jnp.where(lane, pltpu.roll(upper, 64, 1), lower)


def fold(parts):
    return pl.pallas_call(
        fold_kernel,
        out_shape=jax.ShapeDtypeStruct((8, 32, 128), F32),
        in_specs=[pl.BlockSpec(memory_space=pltpu.VMEM)],
        out_specs=pl.BlockSpec(memory_space=pltpu.VMEM),
        compiler_params=pltpu.CompilerParams(vmem_limit_bytes=FOLD_VMEM),
        name="fold",
    )(parts)


def finish_kernel(parts_ref, out_ref):
    total = parts_ref[0]
    for part in range(1, parts_ref.shape[0]):
        total += parts_ref[part]
    block = join([total[:, 0:64], total[:, 64:128]], 0)
    out_ref[...] = block.T


def finish(parts):
    return pl.pallas_call(
        finish_kernel,
        out_shape=jax.ShapeDtypeStruct((64, 64), F32),
        in_specs=[pl.BlockSpec(memory_space=pltpu.VMEM)],
        out_specs=pl.BlockSpec(memory_space=pltpu.VMEM),
        compiler_params=pltpu.CompilerParams(vmem_limit_bytes=FOLD_VMEM),
        name="finish",
    )(parts)


def gain_table(response, norm):
    grid = response.reshape(FAST, SLOW)
    mirror = jnp.concatenate(
        [
            jnp.roll(jnp.flip(grid[:, 0:1], axis=0), 1, axis=0),
            jnp.flip(grid[:, HALF : SLOW], axis=(0, 1)),
        ],
        axis=1,
    )
    even = (grid[:, : HALF + 1] + mirror) * 0.5
    weight = np.full((1, HALF + 1), math.sqrt(2.0))
    weight[0, 0] = weight[0, HALF] = 1.0
    even = even * jnp.asarray((weight / (EPOCHS * norm)).astype(np.float32))
    return jnp.pad(even.T, ((0, KEPT - HALF - 1), (0, 0)))


def exchange(values, axes):
    return lax.all_to_all(values, axes, split_axis=0, concat_axis=0, tiled=True)


def on_device(panel, response):
    fold_tables, turn_tables, inner_tables, spread, norm = host_tables()
    (fold_hi, fold_lo), (inner_hi, inner_lo) = fold_tables, inner_tables
    tables = (
        fold_hi,
        np.concatenate([spread, inner_hi], axis=1),
        np.concatenate([coarse(np.asarray(fold_lo, np.float32) * SHIFT), np.tile(coarse(spread), (1, 2))]),
        np.concatenate([coarse(np.asarray(inner_lo, np.float32) * SHIFT), coarse(inner_hi)]),
        np.concatenate(turn_tables),
    )
    tables = [jnp.asarray(table) for table in tables]
    gain = gain_table(response, norm)
    tables = tuple(settle(table, gain) for table in tables)
    tiles = 2 * FAST // 128
    columns = panel.shape[0] // 16
    series = exchange(panel.reshape(16, columns, -1, FAST), TIMES)
    lines = filter_columns(series, tables, gain)
    lines = exchange(lines.reshape(DEVICES, tiles * columns, 128), EVERY)
    mine = lines.reshape(DEVICES * columns, 2 * FAST)
    other = lax.ppermute(mine, "core", [(0, 1), (1, 0)])
    core = lax.axis_index("core").astype(jnp.int32).reshape(1)
    begun = gram(gram_mine_kernel, (512, 1024), F32, "gram_mine", core, mine)
    part = gram(gram_other_kernel, (16, 64, 512), BF16, "gram_other", core, other, begun)
    folded = exchange(fold(exchange(part, PLANE)), ("z",))
    return finish(folded)


def solution(mesh):
    fine = Mesh(mesh.devices.reshape(2, 4, 2, 8, 2), ("yl", "x", "core", "z", "yh"))
    return jax.shard_map(
        on_device,
        mesh=fine,
        in_specs=(P(ROWS, TIMES), P()),
        out_specs=P(ROWS, TIMES),
        check_vma=False,
    )
```

```python
import math

import jax
import jax.numpy as jnp
import numpy as np
from jax import lax
from jax.experimental import pallas as pl
from jax.experimental.pallas import tpu as pltpu
from jax.sharding import Mesh
from jax.sharding import PartitionSpec as P

EPOCHS = 131072
SLOW = 512
FAST = 256
HALF = SLOW // 2
KEPT = HALF + 8
DEVICES = 256
MIB = 1 << 20
FILTER_VMEM = 10 * MIB
GRAM_VMEM = 24 * MIB
FOLD_VMEM = 16 * MIB

EVERY = ("z", "yh", "yl", "x", "core")
ROWS = ("z", "yh")
TIMES = ("yl", "x", "core")
PLANE = ("yh", "x", "yl")

F32 = jnp.float32
BF16 = jnp.bfloat16
F8 = jnp.float8_e5m2
SHIFT = 256.0
LINE_SHIFT = 65536.0


def split_table(table):
    upper = table.astype(np.float32).astype(BF16)
    lower = (table - upper.astype(np.float64)).astype(np.float32).astype(BF16)
    return upper, lower


def coarse(table):
    return np.asarray(table, np.float32).astype(F8)


def phase(rows, cols, length):
    index = np.outer(np.asarray(rows, np.int64), np.asarray(cols, np.int64)) % length
    return index * (2.0 * math.pi / length)


def host_tables():
    slow = np.arange(SLOW)
    cosine = np.cos(phase(np.arange(HALF + 1), slow, SLOW))
    sine = np.sin(phase(np.arange(1, HALF), slow, SLOW))
    real_fold = np.concatenate([cosine[:HALF], cosine[HALF:], -sine], axis=0)
    turn = phase(np.arange(KEPT), np.arange(FAST), EPOCHS)
    inner = phase(np.arange(FAST), np.arange(FAST), FAST)
    cosine, sine = np.cos(inner), np.sin(inner)
    inner = np.concatenate([cosine, sine - cosine, cosine + sine], axis=1)
    odd = 2 * np.arange(HALF) + 1
    spread = np.cos(phase(odd, odd, 8 * HALF)) * math.sqrt(2.0 / HALF)
    spread_upper, _ = split_table(spread)
    norm = math.sqrt(float((spread_upper.astype(np.float64)[0] ** 2).sum()))
    return (
        split_table(real_fold),
        (np.cos(turn).astype(np.float32), np.sin(turn).astype(np.float32)),
        split_table(inner),
        spread_upper,
        norm,
    )


def dot(left, right):
    return jnp.dot(left, right, preferred_element_type=F32)


def join(parts, axis):
    return jnp.concatenate(parts, axis=axis)


def settle_kernel(table_ref, after_ref, out_ref):
    del table_ref, after_ref, out_ref


def settle(table, after):
    return pl.pallas_call(
        settle_kernel,
        out_shape=jax.ShapeDtypeStruct(table.shape, table.dtype),
        in_specs=[pl.BlockSpec(memory_space=pl.ANY)] * 2,
        out_specs=pl.BlockSpec(memory_space=pl.ANY),
        input_output_aliases={0: 0},
        compiler_params=pltpu.CompilerParams(vmem_limit_bytes=MIB),
        name="settle",
    )(table, after)


def filter_kernel(
    series_ref,
    fold_ref,
    inner_ref,
    coarse_ref,
    rest_ref,
    turn_ref,
    gain_ref,
    out_ref,
):
    fold_hi, fold_lo = fold_ref, coarse_ref.at[0:SLOW]
    spread, spread_lo = inner_ref.at[:, 0:FAST], coarse_ref.at[SLOW : SLOW + HALF, 0:FAST]
    inner_hi = inner_ref.at[:, FAST : 4 * FAST]
    inner_lo = rest_ref
    turn_cos, turn_sin = turn_ref.at[0:KEPT], turn_ref.at[KEPT : 2 * KEPT]
    blocks, columns, runs, _ = series_ref.shape
    first_row = lax.broadcasted_iota(jnp.int32, (HALF, FAST), 0) == 0
    gain = gain_ref[0:HALF, :]
    edge_gain = gain_ref[HALF : HALF + 1, :]
    for column in range(columns):
        series = join([series_ref[j, column] for j in range(blocks)], 0)
        folded = dot(fold_hi[...], series)
        folded += dot(fold_lo[...], series.astype(F8)) * (1 / SHIFT)
        real = folded[0:HALF]
        imag = folded[HALF:SLOW]
        edge = imag[0:1]
        cosine = turn_cos[0:HALF, :]
        sine = turn_sin[0:HALF, :]
        turned_re = real * cosine + imag * sine
        turned_im = jnp.where(first_row, 0.0, imag * cosine - real * sine)
        edge_re = edge * turn_cos[HALF : HALF + 1, :]
        edge_im = -edge * turn_sin[HALF : HALF + 1, :]
        edge_re, edge_im = (jnp.broadcast_to(row, (16, FAST)) for row in (edge_re, edge_im))
        turned_re = join([turned_re, edge_re], 0)
        turned_im = join([turned_im, edge_im], 0)
        products = []
        for index, values in enumerate((turned_re + turned_im, turned_im, turned_re)):
            upper = values.astype(BF16)
            lower = ((values - upper.astype(F32)) * SHIFT).astype(F8)
            lanes = slice(index * FAST, (index + 1) * FAST)
            product = dot(upper, inner_hi[:, lanes])
            coarse_values = join([values.astype(F8), lower], 1)
            products.append(product + dot(coarse_values, inner_lo[:, lanes]) * (1 / SHIFT))
        line_re = products[0] + products[1]
        line_im = products[0] - products[2]
        edge_line = (line_re[HALF : HALF + 1] + line_im[HALF : HALF + 1]) * edge_gain
        line_re = line_re[0:HALF] * gain
        line_im = line_im[0:HALF] * gain
        first = line_re + line_im
        line_re = jnp.where(first_row, first, line_re)
        line_im = jnp.where(first_row, jnp.broadcast_to(edge_line, (HALF, FAST)), line_im)
        packed = join([line_re, line_im], 1)
        upper = packed.astype(BF16)
        lower = ((packed - upper.astype(F32)) * LINE_SHIFT).astype(F8)
        mixed = dot(spread[...], upper) + dot(spread_lo[...], lower) * (1 / LINE_SHIFT)
        out_ref[:, 2 * FAST * column : 2 * FAST * (column + 1)] = mixed.astype(BF16)


def filter_columns(series, tables, gain):
    return pl.pallas_call(
        filter_kernel,
        out_shape=jax.ShapeDtypeStruct((DEVICES, series.shape[1] * 2 * FAST), BF16),
        in_specs=[pl.BlockSpec(memory_space=pltpu.VMEM)] * (len(tables) + 2),
        out_specs=pl.BlockSpec(memory_space=pltpu.VMEM),
        compiler_params=pltpu.CompilerParams(vmem_limit_bytes=FILTER_VMEM),
        cost_estimate=pl.CostEstimate(
            flops=2_000_000_000 * series.shape[1], bytes_accessed=4 * MIB, transcendentals=0
        ),
        name="filter",
    )(series, *tables, gain)


def half_gram(core_ref, ref):
    start = 64 * core_ref[0]
    left = [ref[pl.ds(pl.multiple_of(128 * b + start, 64), 64), :] for b in range(8)]
    right = [ref[64 * b : 64 * b + 64, :] for b in (*range(0, 16, 2), *range(1, 16, 2))]
    return lax.dot_general(
        join(left, 0), join(right, 0), (((1,), (1,)), ((), ())), preferred_element_type=F32
    )


def gram_mine_kernel(core_ref, mine_ref, out_ref):
    out_ref[...] = half_gram(core_ref, mine_ref)


def gram_other_kernel(core_ref, other_ref, begun_ref, out_ref):
    total = (begun_ref[...] + half_gram(core_ref, other_ref)).astype(BF16)
    for block in range(8):
        for parity in range(2):
            out_ref[8 * parity + 2 * (block % 4) + block // 4] = total[
                64 * block : 64 * block + 64, 512 * parity : 512 * parity + 512
            ]


def gram(kernel, shape, dtype, name, core, *arrays):
    return pl.pallas_call(
        kernel,
        out_shape=jax.ShapeDtypeStruct(shape, dtype),
        in_specs=[pl.BlockSpec(memory_space=pltpu.SMEM)]
        + [pl.BlockSpec(memory_space=pltpu.VMEM)] * len(arrays),
        out_specs=pl.BlockSpec(memory_space=pltpu.VMEM),
        compiler_params=pltpu.CompilerParams(vmem_limit_bytes=GRAM_VMEM),
        cost_estimate=pl.CostEstimate(
            flops=1_000_000_000, bytes_accessed=4 * MIB, transcendentals=0
        ),
        name=name,
    )(core, *arrays)


def fold_kernel(parts_ref, out_ref):
    total = parts_ref[0].astype(F32)
    for chip in range(1, parts_ref.shape[0]):
        total += parts_ref[chip].astype(F32)
    lane = lax.broadcasted_iota(jnp.int32, (32, 128), 1) < 64
    for pair in range(4):
        upper = total[0:32, pair * 128 : (pair + 1) * 128]
        lower = total[32:64, pair * 128 : (pair + 1) * 128]
        out_ref[2 * pair] = jnp.where(lane, upper, pltpu.roll(lower, 64, 1))
        out_ref[2 * pair + 1] = jnp.where(lane, pltpu.roll(upper, 64, 1), lower)


def fold(parts):
    return pl.pallas_call(
        fold_kernel,
        out_shape=jax.ShapeDtypeStruct((8, 32, 128), F32),
        in_specs=[pl.BlockSpec(memory_space=pltpu.VMEM)],
        out_specs=pl.BlockSpec(memory_space=pltpu.VMEM),
        compiler_params=pltpu.CompilerParams(vmem_limit_bytes=FOLD_VMEM),
        name="fold",
    )(parts)


def finish_kernel(parts_ref, out_ref):
    total = parts_ref[0]
    for part in range(1, parts_ref.shape[0]):
        total += parts_ref[part]
    block = join([total[:, 0:64], total[:, 64:128]], 0)
    out_ref[...] = block.T


def finish(parts):
    return pl.pallas_call(
        finish_kernel,
        out_shape=jax.ShapeDtypeStruct((64, 64), F32),
        in_specs=[pl.BlockSpec(memory_space=pltpu.VMEM)],
        out_specs=pl.BlockSpec(memory_space=pltpu.VMEM),
        compiler_params=pltpu.CompilerParams(vmem_limit_bytes=FOLD_VMEM),
        name="finish",
    )(parts)


def gain_table(response, norm):
    grid = response.reshape(FAST, SLOW)
    mirror = jnp.concatenate(
        [
            jnp.roll(jnp.flip(grid[:, 0:1], axis=0), 1, axis=0),
            jnp.flip(grid[:, HALF : SLOW], axis=(0, 1)),
        ],
        axis=1,
    )
    even = (grid[:, : HALF + 1] + mirror) * 0.5
    weight = np.full((1, HALF + 1), math.sqrt(2.0))
    weight[0, 0] = weight[0, HALF] = 1.0
    even = even * jnp.asarray((weight / (EPOCHS * norm)).astype(np.float32))
    return jnp.pad(even.T, ((0, KEPT - HALF - 1), (0, 0)))


def exchange(values, axes):
    return lax.all_to_all(values, axes, split_axis=0, concat_axis=0, tiled=True)


def on_device(panel, response):
    fold_tables, turn_tables, inner_tables, spread, norm = host_tables()
    (fold_hi, fold_lo), (inner_hi, inner_lo) = fold_tables, inner_tables
    tables = (
        fold_hi,
        np.concatenate([spread, inner_hi], axis=1),
        np.concatenate([coarse(np.asarray(fold_lo, np.float32) * SHIFT), np.tile(coarse(spread), (1, 2))]),
        np.concatenate([coarse(np.asarray(inner_lo, np.float32) * SHIFT), coarse(inner_hi)]),
        np.concatenate(turn_tables),
    )
    tables = [jnp.asarray(table) for table in tables]
    gain = gain_table(response, norm)
    tables = tuple(settle(table, gain) for table in tables)
    tiles = 2 * FAST // 128
    columns = panel.shape[0] // 16
    series = exchange(panel.reshape(16, columns, -1, FAST), TIMES)
    lines = filter_columns(series, tables, gain)
    lines = exchange(lines.reshape(DEVICES, tiles * columns, 128), EVERY)
    mine = lines.reshape(DEVICES * columns, 2 * FAST)
    other = lax.ppermute(mine, "core", [(0, 1), (1, 0)])
    core = lax.axis_index("core").astype(jnp.int32).reshape(1)
    begun = gram(gram_mine_kernel, (512, 1024), F32, "gram_mine", core, mine)
    part = gram(gram_other_kernel, (16, 64, 512), BF16, "gram_other", core, other, begun)
    folded = exchange(fold(exchange(part, PLANE)), ("z",))
    return finish(folded)


def solution(mesh):
    fine = Mesh(mesh.devices.reshape(2, 4, 2, 8, 2), ("yl", "x", "core", "z", "yh"))
    return jax.shard_map(
        on_device,
        mesh=fine,
        in_specs=(P(ROWS, TIMES), P()),
        out_specs=P(ROWS, TIMES),
        check_vma=False,
    )
```

```python
import math

import jax
import jax.numpy as jnp
import numpy as np
from jax import lax
from jax.experimental import pallas as pl
from jax.experimental.pallas import tpu as pltpu
from jax.sharding import Mesh
from jax.sharding import PartitionSpec as P

EPOCHS = 131072
SLOW = 512
FAST = 256
HALF = SLOW // 2
KEPT = HALF + 8
DEVICES = 256
MIB = 1 << 20
FILTER_VMEM = 10 * MIB
GRAM_VMEM = 24 * MIB
FOLD_VMEM = 16 * MIB

EVERY = ("z", "yh", "yl", "x", "core")
ROWS = ("z", "yh")
TIMES = ("yl", "x", "core")
PLANE = ("yh", "x", "yl")

F32 = jnp.float32
BF16 = jnp.bfloat16
F8 = jnp.float8_e5m2
SHIFT = 256.0
LINE_SHIFT = 65536.0


def split_table(table):
    upper = table.astype(np.float32).astype(BF16)
    lower = (table - upper.astype(np.float64)).astype(np.float32).astype(BF16)
    return upper, lower


def coarse(table):
    return np.asarray(table, np.float32).astype(F8)


def phase(rows, cols, length):
    index = np.outer(np.asarray(rows, np.int64), np.asarray(cols, np.int64)) % length
    return index * (2.0 * math.pi / length)


def host_tables():
    slow = np.arange(SLOW)
    cosine = np.cos(phase(np.arange(HALF + 1), slow, SLOW))
    sine = np.sin(phase(np.arange(1, HALF), slow, SLOW))
    real_fold = np.concatenate([cosine[:HALF], cosine[HALF:], -sine], axis=0)
    turn = phase(np.arange(KEPT), np.arange(FAST), EPOCHS)
    inner = phase(np.arange(FAST), np.arange(FAST), FAST)
    cosine, sine = np.cos(inner), np.sin(inner)
    inner = np.concatenate([cosine, sine - cosine, cosine + sine], axis=1)
    odd = 2 * np.arange(HALF) + 1
    spread = np.cos(phase(odd, odd, 8 * HALF)) * math.sqrt(2.0 / HALF)
    spread_upper, _ = split_table(spread)
    norm = math.sqrt(float((spread_upper.astype(np.float64)[0] ** 2).sum()))
    return (
        split_table(real_fold),
        (np.cos(turn).astype(np.float32), np.sin(turn).astype(np.float32)),
        split_table(inner),
        spread_upper,
        norm,
    )


def dot(left, right):
    return jnp.dot(left, right, preferred_element_type=F32)


def join(parts, axis):
    return jnp.concatenate(parts, axis=axis)


def settle_kernel(table_ref, after_ref, out_ref):
    del table_ref, after_ref, out_ref


def settle(table, after):
    return pl.pallas_call(
        settle_kernel,
        out_shape=jax.ShapeDtypeStruct(table.shape, table.dtype),
        in_specs=[pl.BlockSpec(memory_space=pl.ANY)] * 2,
        out_specs=pl.BlockSpec(memory_space=pl.ANY),
        input_output_aliases={0: 0},
        compiler_params=pltpu.CompilerParams(vmem_limit_bytes=MIB),
        name="settle",
    )(table, after)


def filter_kernel(
    series_ref,
    fold_ref,
    inner_ref,
    coarse_ref,
    rest_ref,
    turn_ref,
    gain_ref,
    out_ref,
):
    fold_hi, fold_lo = fold_ref, coarse_ref.at[0:SLOW]
    spread, spread_lo = inner_ref.at[:, 0:FAST], coarse_ref.at[SLOW : SLOW + HALF, 0:FAST]
    inner_hi = inner_ref.at[:, FAST : 4 * FAST]
    inner_lo = rest_ref
    turn_cos, turn_sin = turn_ref.at[0:KEPT], turn_ref.at[KEPT : 2 * KEPT]
    blocks, columns, runs, _ = series_ref.shape
    first_row = lax.broadcasted_iota(jnp.int32, (HALF, FAST), 0) == 0
    gain = gain_ref[0:HALF, :]
    edge_gain = gain_ref[HALF : HALF + 1, :]
    for column in range(columns):
        series = join([series_ref[j, column] for j in range(blocks)], 0)
        folded = dot(fold_hi[...], series)
        folded += dot(fold_lo[...], series.astype(F8)) * (1 / SHIFT)
        real = folded[0:HALF]
        imag = folded[HALF:SLOW]
        edge = imag[0:1]
        cosine = turn_cos[0:HALF, :]
        sine = turn_sin[0:HALF, :]
        turned_re = real * cosine + imag * sine
        turned_im = jnp.where(first_row, 0.0, imag * cosine - real * sine)
        edge_re = edge * turn_cos[HALF : HALF + 1, :]
        edge_im = -edge * turn_sin[HALF : HALF + 1, :]
        edge_re, edge_im = (jnp.broadcast_to(row, (16, FAST)) for row in (edge_re, edge_im))
        turned_re = join([turned_re, edge_re], 0)
        turned_im = join([turned_im, edge_im], 0)
        products = []
        for index, values in enumerate((turned_re + turned_im, turned_im, turned_re)):
            upper = values.astype(BF16)
            lower = ((values - upper.astype(F32)) * SHIFT).astype(F8)
            lanes = slice(index * FAST, (index + 1) * FAST)
            product = dot(upper, inner_hi[:, lanes])
            coarse_values = join([values.astype(F8), lower], 1)
            products.append(product + dot(coarse_values, inner_lo[:, lanes]) * (1 / SHIFT))
        line_re = products[0] + products[1]
        line_im = products[0] - products[2]
        edge_line = (line_re[HALF : HALF + 1] + line_im[HALF : HALF + 1]) * edge_gain
        line_re = line_re[0:HALF] * gain
        line_im = line_im[0:HALF] * gain
        first = line_re + line_im
        line_re = jnp.where(first_row, first, line_re)
        line_im = jnp.where(first_row, jnp.broadcast_to(edge_line, (HALF, FAST)), line_im)
        packed = join([line_re, line_im], 1)
        upper = packed.astype(BF16)
        lower = ((packed - upper.astype(F32)) * LINE_SHIFT).astype(F8)
        mixed = dot(spread[...], upper) + dot(spread_lo[...], lower) * (1 / LINE_SHIFT)
        out_ref[:, 2 * FAST * column : 2 * FAST * (column + 1)] = mixed.astype(BF16)


def filter_columns(series, tables, gain):
    return pl.pallas_call(
        filter_kernel,
        out_shape=jax.ShapeDtypeStruct((DEVICES, series.shape[1] * 2 * FAST), BF16),
        in_specs=[pl.BlockSpec(memory_space=pltpu.VMEM)] * (len(tables) + 2),
        out_specs=pl.BlockSpec(memory_space=pltpu.VMEM),
        compiler_params=pltpu.CompilerParams(vmem_limit_bytes=FILTER_VMEM),
        cost_estimate=pl.CostEstimate(
            flops=2_000_000_000 * series.shape[1], bytes_accessed=4 * MIB, transcendentals=0
        ),
        name="filter",
    )(series, *tables, gain)


def half_gram(core_ref, ref):
    start = 64 * core_ref[0]
    left = [ref[pl.ds(pl.multiple_of(128 * b + start, 64), 64), :] for b in range(8)]
    right = [ref[64 * b : 64 * b + 64, :] for b in (*range(0, 16, 2), *range(1, 16, 2))]
    return lax.dot_general(
        join(left, 0), join(right, 0), (((1,), (1,)), ((), ())), preferred_element_type=F32
    )


def gram_mine_kernel(core_ref, mine_ref, out_ref):
    out_ref[...] = half_gram(core_ref, mine_ref)


def gram_other_kernel(core_ref, other_ref, begun_ref, out_ref):
    total = (begun_ref[...] + half_gram(core_ref, other_ref)).astype(BF16)
    for block in range(8):
        for parity in range(2):
            out_ref[8 * parity + 2 * (block % 4) + block // 4] = total[
                64 * block : 64 * block + 64, 512 * parity : 512 * parity + 512
            ]


def gram(kernel, shape, dtype, name, core, *arrays):
    return pl.pallas_call(
        kernel,
        out_shape=jax.ShapeDtypeStruct(shape, dtype),
        in_specs=[pl.BlockSpec(memory_space=pltpu.SMEM)]
        + [pl.BlockSpec(memory_space=pltpu.VMEM)] * len(arrays),
        out_specs=pl.BlockSpec(memory_space=pltpu.VMEM),
        compiler_params=pltpu.CompilerParams(vmem_limit_bytes=GRAM_VMEM),
        cost_estimate=pl.CostEstimate(
            flops=1_000_000_000, bytes_accessed=4 * MIB, transcendentals=0
        ),
        name=name,
    )(core, *arrays)


def fold_kernel(parts_ref, out_ref):
    total = parts_ref[0].astype(F32)
    for chip in range(1, parts_ref.shape[0]):
        total += parts_ref[chip].astype(F32)
    lane = lax.broadcasted_iota(jnp.int32, (32, 128), 1) < 64
    for pair in range(4):
        upper = total[0:32, pair * 128 : (pair + 1) * 128]
        lower = total[32:64, pair * 128 : (pair + 1) * 128]
        out_ref[2 * pair] = jnp.where(lane, upper, pltpu.roll(lower, 64, 1)).astype(BF16)
        out_ref[2 * pair + 1] = jnp.where(lane, pltpu.roll(upper, 64, 1), lower).astype(BF16)


def fold(parts):
    return pl.pallas_call(
        fold_kernel,
        out_shape=jax.ShapeDtypeStruct((8, 32, 128), BF16),
        in_specs=[pl.BlockSpec(memory_space=pltpu.VMEM)],
        out_specs=pl.BlockSpec(memory_space=pltpu.VMEM),
        compiler_params=pltpu.CompilerParams(vmem_limit_bytes=FOLD_VMEM),
        name="fold",
    )(parts)


def finish_kernel(parts_ref, out_ref):
    total = parts_ref[0].astype(F32)
    for part in range(1, parts_ref.shape[0]):
        total += parts_ref[part].astype(F32)
    block = join([total[:, 0:64], total[:, 64:128]], 0)
    out_ref[...] = block.T


def finish(parts):
    return pl.pallas_call(
        finish_kernel,
        out_shape=jax.ShapeDtypeStruct((64, 64), F32),
        in_specs=[pl.BlockSpec(memory_space=pltpu.VMEM)],
        out_specs=pl.BlockSpec(memory_space=pltpu.VMEM),
        compiler_params=pltpu.CompilerParams(vmem_limit_bytes=FOLD_VMEM),
        name="finish",
    )(parts)


def gain_table(response, norm):
    grid = response.reshape(FAST, SLOW)
    mirror = jnp.concatenate(
        [
            jnp.roll(jnp.flip(grid[:, 0:1], axis=0), 1, axis=0),
            jnp.flip(grid[:, HALF : SLOW], axis=(0, 1)),
        ],
        axis=1,
    )
    even = (grid[:, : HALF + 1] + mirror) * 0.5
    weight = np.full((1, HALF + 1), math.sqrt(2.0))
    weight[0, 0] = weight[0, HALF] = 1.0
    even = even * jnp.asarray((weight / (EPOCHS * norm)).astype(np.float32))
    return jnp.pad(even.T, ((0, KEPT - HALF - 1), (0, 0)))


def exchange(values, axes):
    return lax.all_to_all(values, axes, split_axis=0, concat_axis=0, tiled=True)


def on_device(panel, response):
    fold_tables, turn_tables, inner_tables, spread, norm = host_tables()
    (fold_hi, fold_lo), (inner_hi, inner_lo) = fold_tables, inner_tables
    tables = (
        fold_hi,
        np.concatenate([spread, inner_hi], axis=1),
        np.concatenate([coarse(np.asarray(fold_lo, np.float32) * SHIFT), np.tile(coarse(spread), (1, 2))]),
        np.concatenate([coarse(np.asarray(inner_lo, np.float32) * SHIFT), coarse(inner_hi)]),
        np.concatenate(turn_tables),
    )
    tables = [jnp.asarray(table) for table in tables]
    gain = gain_table(response, norm)
    tables = tuple(settle(table, gain) for table in tables)
    tiles = 2 * FAST // 128
    columns = panel.shape[0] // 16
    series = exchange(panel.reshape(16, columns, -1, FAST), TIMES)
    lines = filter_columns(series, tables, gain)
    lines = exchange(lines.reshape(DEVICES, tiles * columns, 128), EVERY)
    mine = lines.reshape(DEVICES * columns, 2 * FAST)
    other = lax.ppermute(mine, "core", [(0, 1), (1, 0)])
    core = lax.axis_index("core").astype(jnp.int32).reshape(1)
    begun = gram(gram_mine_kernel, (512, 1024), F32, "gram_mine", core, mine)
    part = gram(gram_other_kernel, (16, 64, 512), BF16, "gram_other", core, other, begun)
    folded = exchange(fold(exchange(part, PLANE)), ("z",))
    return finish(folded)


def solution(mesh):
    fine = Mesh(mesh.devices.reshape(2, 4, 2, 8, 2), ("yl", "x", "core", "z", "yh"))
    return jax.shard_map(
        on_device,
        mesh=fine,
        in_specs=(P(ROWS, TIMES), P()),
        out_specs=P(ROWS, TIMES),
        check_vma=False,
    )
```
